32 devices in a mesh: wide: 2 (over x), grow: 4 (over y, core), gcol: 4 (over z).
Axes of the slice: x: 2, y: 2, z: 4, core: 2. Of those that a mesh axis runs over, the one named last changes fastest.
Arguments:
- diag_block: float32 [2, 1024, 1024], P('wide', ('grow', 'gcol')), as said below
- lower_block: float32 [2, 3072, 1024], P('wide', ('grow', 'gcol')), may hold values from -0.1875 to 0.1875
- trailing_block: float32 [2, 3072, 3072], P('wide', 'grow', 'gcol'), as said below
- parent_front: float32 [4, 2048, 8192], P('grow', 'wide', 'gcol'), may hold values from -3 to 3
- row_map: int32 [2, 24], replicated, may hold values from 0 to 63, as said below
Outputs:
- factor: float32 [2, 1024, 1024], P('wide', ('grow', 'gcol'))
- panel: float32 [2, 3072, 1024], P('wide', ('grow', 'gcol'))
- parent: float32 [4, 2048, 8192], P('grow', 'wide', 'gcol')
The draws below stay inside these ranges and needn't reach their ends.
Inputs may be any that keep to these rules, and one draw needn't show every extreme that they name: Each diag_block[g] is symmetric and positive definite. Each trailing_block[g] is symmetric. `row_map`: the blocks of one child are distinct, and child block b goes to a grandparent block p with p // 16 equal to b // 6.
All inputs are finite; a program needn't handle non-finite values.
Results may differ from the reference program's by a relative error of at most 0.0003.
Values sent between devices are 32-bit elements; how exact they have to be, the bound alone decides.
A program may use at most 128 MiB of HBM per device.

```python
import jax
import jax.numpy as jnp
from jax import lax

NS = 1024
NC = 3072
PN = 8192
BLOCK = 128
GROUPS = 2
QUARTERS = 4
PQ = 2048


def draw_diag_block(key, part):
    noise = jax.random.normal(key, (GROUPS, NS, NS), jnp.float32)
    sym = (noise + jnp.swapaxes(noise, 1, 2)) * (0.5 / NS ** 0.5)
    base = 2.5 + jax.random.uniform(jax.random.fold_in(key, 1), (GROUPS, NS), jnp.float32, 0.0, 1.5)
    matrix = sym + base[:, :, None] * jnp.eye(NS, dtype=jnp.float32)[None]
    return matrix


def draw_trailing_block(key, part):
    noise = jax.random.normal(key, (GROUPS, NC, NC), jnp.float32)
    sym = (noise + jnp.swapaxes(noise, 1, 2)) * (0.5 / NC ** 0.5)
    base = jax.random.uniform(jax.random.fold_in(key, 1), (GROUPS, NC), jnp.float32, 0.5, 1.5)
    return sym + base[:, :, None] * jnp.eye(NC, dtype=jnp.float32)[None]


def draw_row_map(key, part):
    quarter_blocks = PN // (BLOCK * QUARTERS)
    child_blocks = NC // (BLOCK * QUARTERS)
    keys = jax.random.split(jax.random.fold_in(key, 7), GROUPS * QUARTERS)
    orders = jax.vmap(lambda single: jax.random.permutation(single, quarter_blocks))(keys)
    picked = orders[:, :child_blocks].reshape(GROUPS, QUARTERS, child_blocks)
    shifted = picked + (jnp.arange(QUARTERS, dtype=jnp.int32) * quarter_blocks)[None, :, None]
    return shifted.reshape(GROUPS, QUARTERS * child_blocks).astype(jnp.int32)


def levels(rng, dims, cuts, least, largest):
    level = 1.0
    for dim, parts in cuts:
        steps = jax.random.uniform(jax.random.fold_in(jax.random.fold_in(rng, 6), dim), (parts,), jnp.float32, least / len(cuts), largest / len(cuts))
        level = level * jnp.repeat(jnp.exp(steps), dims[dim] // parts).reshape((-1,) + (1,) * (len(dims) - 1 - dim))
    return level


def gaussian(own_key, shape, width, reach, shards=(), kind=jnp.bfloat16):
    factor_of = levels(own_key, shape, shards, -0.22, 0.18) if shards else 1.0
    values = jax.random.normal(own_key, shape, jnp.float32) * width * factor_of
    return jnp.minimum(jnp.maximum(values, -reach), reach).astype(kind)


def setup_inputs(seed: int = 0) -> dict:
    arg_keys = jax.random.split(jax.random.key(seed), 6)
    diag_block = draw_diag_block(jax.random.fold_in(arg_keys[5], 71), 0)
    lower_block = gaussian(arg_keys[1], (GROUPS, NC, NS), NS ** -0.5, 0.1875, ((0, 2), (1, 16)), jnp.float32)
    trailing_block = draw_trailing_block(jax.random.fold_in(arg_keys[5], 71), 0)
    parent_front = gaussian(arg_keys[3], (QUARTERS, PQ, PN), 0.5, 3.0, ((0, 4), (1, 2), (2, 4)), jnp.float32)
    row_map = draw_row_map(jax.random.fold_in(arg_keys[5], 71), 0)
    return {"diag_block": diag_block, "lower_block": lower_block, "trailing_block": trailing_block, "parent_front": parent_front, "row_map": row_map}


def reference(diag_block, lower_block, trailing_block, parent_front, row_map):
    factor = jnp.linalg.cholesky(diag_block)
    solved = jax.scipy.linalg.solve_triangular(factor, jnp.swapaxes(lower_block, 1, 2), lower=True)
    panel = jnp.swapaxes(solved, 1, 2)
    schur = trailing_block - jnp.einsum('gik,gjk->gij', panel, panel, precision=lax.Precision.HIGHEST)
    order = parent_front.shape[0] * parent_front.shape[1]
    offsets = jnp.arange(BLOCK, dtype=jnp.int32)

    def add_child(total, item):
        contribution, blocks = item
        index = (blocks.astype(jnp.int32)[:, None] * BLOCK + offsets[None, :]).reshape(-1)
        return (total.at[index[:, None], index[None, :]].add(contribution), None)
    total, _ = lax.scan(add_child, parent_front.reshape(order, order), (schur, row_map))
    return (factor, panel, total.reshape(parent_front.shape))
```

```python
import functools

import jax
import jax.numpy as jnp
from jax import lax
from jax.experimental import pallas as pl
from jax.experimental.pallas import tpu as pltpu
from jax.sharding import PartitionSpec as P

BLOCK = 128
HALF = 64
F32 = jnp.float32
BF16 = jnp.bfloat16
NT = (((1,), (1,)), ((), ()))
NN = (((1,), (0,)), ((), ()))
VMEM = pl.BlockSpec(memory_space=pltpu.VMEM)
SMEM = pl.BlockSpec(memory_space=pltpu.SMEM)


def full_dot(a, b, dims):
    return lax.dot_general(
        a, b, dims, precision=lax.Precision.HIGHEST, preferred_element_type=F32
    )


def parts(x):
    high = x.astype(BF16)
    return high, (x - high.astype(F32)).astype(BF16)


def split_dot(a, b, dims):
    one = functools.partial(lax.dot_general, dimension_numbers=dims, preferred_element_type=F32)
    return one(a[0], b[0]) + (one(a[0], b[1]) + one(a[1], b[0]))


def factor_half(block):
    half = block.shape[0]
    rows = lax.broadcasted_iota(jnp.int32, (half, half), 0)
    cols = lax.broadcasted_iota(jnp.int32, (half, half), 1)
    eye = jnp.where(rows == cols, 1.0, 0.0).astype(F32)
    full = jnp.concatenate([block, eye], axis=1)
    count = half // 8
    wide = (8, 2 * half)
    groups = [full[8 * s : 8 * s + 8] for s in range(count)]
    sub = lax.broadcasted_iota(jnp.int32, wide, 0)
    done = []
    for s in range(count):
        c = 8 * s
        spread = lambda x: jnp.broadcast_to(x, wide)
        lead = [spread(groups[s][i : i + 1, :]) for i in range(8)]
        pivot = {
            (i, j): spread(lead[i][:, c + j : c + j + 1]) for i in range(8) for j in range(i, 8)
        }
        below = range(s + 1, count)
        column = {t: [spread(groups[t][:, c + j : c + j + 1]) for j in range(8)] for t in below}
        keep = jnp.zeros(wide, F32)
        for j in range(8):
            r = lax.rsqrt(pivot[j, j])
            unit = lead[j] * r
            mult = {i: pivot[j, i] * r for i in range(j + 1, 8)}
            for i in range(j + 1, 8):
                for q in range(i, 8):
                    pivot[i, q] = pivot[i, q] - mult[i] * mult[q]
                lead[i] = lead[i] - mult[i] * unit
            for t in below:
                m = column[t][j] * r
                for i in range(j + 1, 8):
                    column[t][i] = column[t][i] - m * mult[i]
                groups[t] = groups[t] - m * unit
            keep = jnp.where(sub == j, unit, keep)
        done.append(keep)
    both = jnp.concatenate(done, axis=0)
    upper = jnp.where(rows <= cols, both[:, :half], 0.0)
    inverse = jnp.where(rows >= cols, both[:, half:], 0.0)
    return upper.T, inverse


def square(a, b, c):
    return jnp.concatenate(
        [
            jnp.concatenate([a, jnp.zeros_like(a)], axis=1),
            jnp.concatenate([b, c], axis=1),
        ],
        axis=0,
    )


def factor_in_place(a, w):
    n = a.shape[0]
    count = n // BLOCK

    def step(k, carry):
        o = pl.multiple_of(k * BLOCK, BLOCK)
        d = a[pl.ds(o, BLOCK), pl.ds(o, BLOCK)]
        l1, w1 = factor_half(d[:HALF, :HALF])
        l21 = full_dot(d[HALF:, :HALF], w1, NT)
        l2, w2 = factor_half(d[HALF:, HALF:] - full_dot(l21, l21, NT))
        w21 = -full_dot(w2, full_dot(l21, w1, NN), NN)
        a[pl.ds(o, BLOCK), pl.ds(o, BLOCK)] = square(l1, l21, l2)
        w[k] = square(w1, w21, w2)
        for at in range(count - 1):

            @pl.when(k == at)
            def _(at=at):
                low, high = at * BLOCK, at * BLOCK + BLOCK
                a[low:high, high:] = jnp.zeros((BLOCK, n - high), F32)
                p = full_dot(a[high:, low:high], w[at], NT)
                a[high:, low:high] = p
                for c in range(high, n, 2 * BLOCK):
                    e = min(c + 2 * BLOCK, n)
                    a[c:, c:e] = a[c:, c:e] - full_dot(p[c - high :], p[c - high : e - high], NT)

        return carry

    lax.fori_loop(0, count, step, 0)


def factor_kernel(x_ref, l_ref, w_ref):
    l_ref[...] = x_ref[...]
    factor_in_place(l_ref, w_ref)


def factor_call(whole):
    n = whole.shape[0]
    return pl.pallas_call(
        factor_kernel,
        name="factor",
        out_shape=(
            jax.ShapeDtypeStruct((n, n), F32),
            jax.ShapeDtypeStruct((n // BLOCK, BLOCK, BLOCK), F32),
        ),
        in_specs=[VMEM],
        out_specs=(VMEM, VMEM),
        compiler_params=pltpu.CompilerParams(vmem_limit_bytes=40 << 20),
        cost_estimate=pl.CostEstimate(flops=n**3 * 20, bytes_accessed=8 * n * n, transcendentals=0),
    )(whole)


def update_kernel(
    owners, slots, quarter, map_ref, l_ref, w_ref, br_ref, bc_ref, t_ref,
    panel_ref, out_ref, source_ref, xh, xl, lh, ll,
):
    n = l_ref.shape[0]
    q = br_ref.shape[0]
    share = panel_ref.shape[0]
    child = lax.axis_index("wide")
    row = lax.axis_index("grow")
    column = lax.axis_index("gcol")
    blocks = q // BLOCK
    per_owner = quarter // owners
    tile = 2 * BLOCK
    sides = (br_ref, bc_ref)
    lh[...], ll[...] = parts(l_ref[...])
    for k in range(n // BLOCK):
        low, high = k * BLOCK, k * BLOCK + BLOCK
        wk = parts(w_ref[k])

        def solve(i, carry, low=low, high=high, wk=wk):
            o = pl.multiple_of(i * tile, tile)
            for side, b in enumerate(sides):
                rest = b[pl.ds(o, tile), low:high]
                at = pl.ds(side * q + o, tile)
                if low:
                    rest = rest - split_dot(
                        (xh[at, :low], xl[at, :low]), (lh[low:high, :low], ll[low:high, :low]), NT
                    )
                x = split_dot(parts(rest), wk, NT)
                xh[at, low:high], xl[at, low:high] = parts(x)
                if side == 0:
                    br_ref[pl.ds(o, tile), low:high] = x
            return carry

        lax.fori_loop(0, q // tile, solve, 0)
    panel_ref[...] = br_ref[pl.ds(pl.multiple_of(column * share, share), share), :]

    def clear(i, carry):
        source_ref[i] = -1
        return carry

    lax.fori_loop(0, owners * per_owner, clear, 0)

    def place(g, carry):
        for b in range(blocks):
            to = map_ref[g, row * blocks + b] % quarter
            rank = jnp.int32(0)
            for e in range(b):
                other = map_ref[g, row * blocks + e] % quarter
                rank += (other // per_owner == to // per_owner).astype(jnp.int32)

            @pl.when(to // per_owner == child)
            def _(to=to, rank=rank):
                source_ref[g * per_owner + to % per_owner] = rank

        return carry

    lax.fori_loop(0, owners, place, 0)

    for b in range(blocks):
        o = b * BLOCK
        to = (map_ref[child, row * blocks + b] % quarter) // per_owner
        rank = jnp.int32(0)
        for e in range(b):
            other = (map_ref[child, row * blocks + e] % quarter) // per_owner
            rank += (other == to).astype(jnp.int32)
        out_ref[to * slots + rank] = t_ref[o : o + BLOCK, :] - split_dot(
            (xh[o : o + BLOCK, :], xl[o : o + BLOCK, :]), (xh[q:, :], xl[q:, :]), NT
        )


def update_call(row_map, factor, inverses, b_row, b_col, trailing, share, owners, slots, quarter):
    n = factor.shape[0]
    q = b_row.shape[0]
    return pl.pallas_call(
        functools.partial(update_kernel, owners, slots, quarter),
        name="update",
        out_shape=(
            jax.ShapeDtypeStruct((share, n), F32),
            jax.ShapeDtypeStruct((owners * slots, BLOCK, q), F32),
            jax.ShapeDtypeStruct((quarter,), jnp.int32),
        ),
        in_specs=[SMEM] + [VMEM] * 5,
        out_specs=(VMEM, VMEM, SMEM),
        scratch_shapes=[
            pltpu.VMEM((2 * q, n), BF16),
            pltpu.VMEM((2 * q, n), BF16),
            pltpu.VMEM((n, n), BF16),
            pltpu.VMEM((n, n), BF16),
        ],
        compiler_params=pltpu.CompilerParams(vmem_limit_bytes=56 << 20),
    )(row_map, factor, inverses, b_row, b_col, trailing)


def add_kernel(owners, map_ref, source_ref, parent_ref, in_ref, out_ref):
    p, g = pl.program_id(0), pl.program_id(1)
    per_owner = pl.num_programs(0)
    blocks = in_ref.shape[2] // BLOCK
    column_blocks = out_ref.shape[2] // BLOCK
    column = lax.axis_index("gcol")

    @pl.when(g == 0)
    def _():
        out_ref[...] = parent_ref[...]

    @pl.when(source_ref[g * per_owner + p] >= 0)
    def _():
        for b in range(blocks):
            to = map_ref[g, column * blocks + b] % column_blocks
            at = pl.ds(pl.multiple_of(to * BLOCK, BLOCK), BLOCK)
            out_ref[0, :, at] += in_ref[0, :, b * BLOCK : b * BLOCK + BLOCK]


def add_call(row_map, source, parent, incoming, owners, slots):
    _, rows, width = parent.shape
    per_owner = rows // BLOCK

    def pick(p, g, map_ref, source_ref):
        return (g * slots + jnp.maximum(source_ref[g * per_owner + p], 0), 0, 0)

    block = pl.BlockSpec((1, BLOCK, width), lambda p, g, *_: (0, p, 0))
    return pl.pallas_call(
        functools.partial(add_kernel, owners),
        name="extend_add",
        out_shape=jax.ShapeDtypeStruct(parent.shape, F32),
        grid_spec=pltpu.PrefetchScalarGridSpec(
            num_scalar_prefetch=2,
            grid=(per_owner, owners),
            in_specs=[block, pl.BlockSpec((1, BLOCK, incoming.shape[2]), pick)],
            out_specs=block,
        ),
        compiler_params=pltpu.CompilerParams(vmem_limit_bytes=32 << 20),
    )(row_map, source, parent, incoming)


def body(diag_block, lower_block, trailing_block, parent_front, row_map):
    owners = lax.axis_size("wide")
    rows, columns = lax.axis_size("grow"), lax.axis_size("gcol")
    share = diag_block.shape[1]
    row, column = lax.axis_index("grow"), lax.axis_index("gcol")
    whole = lax.all_gather(diag_block[0], ("grow", "gcol"), axis=0, tiled=True)
    b_row = lax.all_gather(lower_block[0], "gcol", axis=0, tiled=True)
    turn = [(a * columns + b, b * columns + a) for a in range(rows) for b in range(columns)]
    b_col = lax.ppermute(b_row, ("grow", "gcol"), turn)
    factor, inverses = factor_call(whole)
    factor_rows = lax.dynamic_slice_in_dim(factor, (row * columns + column) * share, share, 0)
    quarter = parent_front.shape[1] * owners // BLOCK
    blocks = trailing_block.shape[1] // BLOCK
    slots = min(blocks, quarter // owners)
    panel, outgoing, source = update_call(
        row_map, factor, inverses, b_row, b_col, trailing_block[0],
        lower_block.shape[1], owners, slots, quarter,
    )
    incoming = lax.all_to_all(outgoing, "wide", split_axis=0, concat_axis=0, tiled=True)
    parent = add_call(row_map, source, parent_front, incoming, owners, slots)
    return (factor_rows[None], panel[None], parent)


def solution(mesh):
    placed = (
        P("wide", ("grow", "gcol"), None),
        P("wide", ("grow", "gcol"), None),
        P("wide", "grow", "gcol"),
        P("grow", "wide", "gcol"),
        P(),
    )
    return jax.shard_map(
        body,
        mesh=mesh,
        in_specs=placed,
        out_specs=(
            P("wide", ("grow", "gcol"), None),
            P("wide", ("grow", "gcol"), None),
            P("grow", "wide", "gcol"),
        ),
        check_vma=False,
    )
```

```python
import functools

import jax
import jax.numpy as jnp
from jax import lax
from jax.experimental import pallas as pl
from jax.experimental.pallas import tpu as pltpu
from jax.sharding import PartitionSpec as P

BLOCK = 128
HALF = 64
F32 = jnp.float32
BF16 = jnp.bfloat16
NT = (((1,), (1,)), ((), ()))
NN = (((1,), (0,)), ((), ()))
VMEM = pl.BlockSpec(memory_space=pltpu.VMEM)
SMEM = pl.BlockSpec(memory_space=pltpu.SMEM)


def full_dot(a, b, dims):
    return lax.dot_general(
        a, b, dims, precision=lax.Precision.HIGHEST, preferred_element_type=F32
    )


def parts(x):
    high = x.astype(BF16)
    return high, (x - high.astype(F32)).astype(BF16)


def split_dot(a, b, dims):
    one = functools.partial(lax.dot_general, dimension_numbers=dims, preferred_element_type=F32)
    return one(a[0], b[0]) + (one(a[0], b[1]) + one(a[1], b[0]))


def factor_half(block):
    half = block.shape[0]
    rows = lax.broadcasted_iota(jnp.int32, (half, half), 0)
    cols = lax.broadcasted_iota(jnp.int32, (half, half), 1)
    eye = jnp.where(rows == cols, 1.0, 0.0).astype(F32)
    full = jnp.concatenate([block, eye], axis=1)
    count = half // 8
    wide = (8, 2 * half)
    groups = [full[8 * s : 8 * s + 8] for s in range(count)]
    sub = lax.broadcasted_iota(jnp.int32, wide, 0)
    done = []
    for s in range(count):
        c = 8 * s
        spread = lambda x: jnp.broadcast_to(x, wide)
        lead = [spread(groups[s][i : i + 1, :]) for i in range(8)]
        pivot = {
            (i, j): spread(lead[i][:, c + j : c + j + 1]) for i in range(8) for j in range(i, 8)
        }
        below = range(s + 1, count)
        column = {t: [spread(groups[t][:, c + j : c + j + 1]) for j in range(8)] for t in below}
        keep = jnp.zeros(wide, F32)
        for j in range(8):
            r = lax.rsqrt(pivot[j, j])
            unit = lead[j] * r
            mult = {i: pivot[j, i] * r for i in range(j + 1, 8)}
            for i in range(j + 1, 8):
                for q in range(i, 8):
                    pivot[i, q] = pivot[i, q] - mult[i] * mult[q]
                lead[i] = lead[i] - mult[i] * unit
            for t in below:
                m = column[t][j] * r
                for i in range(j + 1, 8):
                    column[t][i] = column[t][i] - m * mult[i]
                groups[t] = groups[t] - m * unit
            keep = jnp.where(sub == j, unit, keep)
        done.append(keep)
    both = jnp.concatenate(done, axis=0)
    upper = jnp.where(rows <= cols, both[:, :half], 0.0)
    inverse = jnp.where(rows >= cols, both[:, half:], 0.0)
    return upper.T, inverse


def square(a, b, c):
    return jnp.concatenate(
        [
            jnp.concatenate([a, jnp.zeros_like(a)], axis=1),
            jnp.concatenate([b, c], axis=1),
        ],
        axis=0,
    )


def factor_in_place(a, w, between):
    n = a.shape[0]
    count = n // BLOCK

    def step(k, carry):
        o = pl.multiple_of(k * BLOCK, BLOCK)
        d = a[pl.ds(o, BLOCK), pl.ds(o, BLOCK)]
        l1, w1 = factor_half(d[:HALF, :HALF])
        l21 = full_dot(d[HALF:, :HALF], w1, NT)
        l2, w2 = factor_half(d[HALF:, HALF:] - full_dot(l21, l21, NT))
        w21 = -full_dot(w2, full_dot(l21, w1, NN), NN)
        a[pl.ds(o, BLOCK), pl.ds(o, BLOCK)] = square(l1, l21, l2)
        w[k] = square(w1, w21, w2)
        for at in range(count - 1):

            @pl.when(k == at)
            def _(at=at):
                low, high = at * BLOCK, at * BLOCK + BLOCK
                a[low:high, high:] = jnp.zeros((BLOCK, n - high), F32)
                p = full_dot(a[high:, low:high], w[at], NT)
                a[high:, low:high] = p
                for c in range(high, n, 2 * BLOCK):
                    e = min(c + 2 * BLOCK, n)
                    a[c:, c:e] = a[c:, c:e] - full_dot(p[c - high :], p[c - high : e - high], NT)
                for act in between.get(at, ()):
                    act()

        return carry

    lax.fori_loop(0, count, step, 0)


def gather_factor_kernel(
    rows, columns, d_ref, x_ref, a, w, br, bc,
    local, line_send, line_recv, far_send, far_recv, near_send, near_recv,
    b_send, b_recv, c_send, c_recv,
):
    row, column = lax.axis_index("grow"), lax.axis_index("gcol")
    far_row = lax.rem(row + rows // 2, rows)
    near_row = row + 1 - 2 * lax.rem(row, 2)
    right, left = {"gcol": column + 1}, {"gcol": column - 1}
    far, near = {"grow": far_row}, {"grow": near_row}
    share, part = d_ref.shape[0], x_ref.shape[0]
    has_left, has_right = column > 0, column < columns - 1

    def band(r, c):
        return a.at[pl.ds(pl.multiple_of((r * columns + c) * share, share), share)]

    def piece(ref, c):
        return ref.at[pl.ds(pl.multiple_of(c * part, part), part)]

    def remote(ref, send, recv, to):
        return pltpu.make_async_remote_copy(
            src_ref=ref, dst_ref=ref, send_sem=send, recv_sem=recv,
            device_id=to, device_id_type=pl.DeviceIdType.MESH,
        )

    own_d = pltpu.make_async_copy(d_ref, band(row, column), local.at[0])
    own_x = pltpu.make_async_copy(x_ref, piece(br, column), local.at[1])
    own_d.start()
    own_x.start()
    barrier = pltpu.get_barrier_semaphore()
    next_column = {"gcol": lax.rem(column + 1, columns)}
    last_column = {"gcol": lax.rem(column + columns - 1, columns)}
    for to in (far, near, next_column, last_column):
        pl.semaphore_signal(barrier, inc=1, device_id=to, device_id_type=pl.DeviceIdType.MESH)
    pl.semaphore_wait(barrier, 4)
    own_d.wait()
    own_x.wait()

    def pass_on(ref, send, recv, c, both=False):
        @pl.when((c <= column) & has_right)
        def _():
            remote(ref, send.at[0, c], recv.at[c], right).start()

        @pl.when((c >= column) & has_left)
        def _():
            remote(ref, send.at[1, c], recv.at[c], left).start()

    def passed(ref, send, recv, c):
        @pl.when((c <= column) & has_right)
        def _():
            remote(ref, send.at[0, c], recv.at[c], right).wait_send()

        @pl.when((c >= column) & has_left)
        def _():
            remote(ref, send.at[1, c], recv.at[c], left).wait_send()

    def at_distance(d, act):
        for c, there in ((column - d, column - d >= 0), (column + d, column + d < columns)):
            pl.when(there)(functools.partial(act, c))

    def spread(c):
        remote(band(row, c), far_send.at[c], far_recv.at[c], far).start()
        remote(band(row, c), near_send.at[0, c], near_recv.at[0, c], near).start()

    pass_on(band(row, column), line_send, line_recv, column)
    spread(column)

    def arrived(c):
        remote(band(row, c), line_send.at[0, c], line_recv.at[c], right).wait_recv()
        pass_on(band(row, c), line_send, line_recv, c)
        spread(c)

    def crossed(c):
        remote(band(far_row, c), far_send.at[c], far_recv.at[c], far).wait_recv()
        remote(band(far_row, c), near_send.at[1, c], near_recv.at[1, c], near).start()

    at_distance(1, arrived)
    crossed(column)
    for d in range(2, columns):
        at_distance(d, arrived)
        at_distance(d - 1, crossed)
    pass_on(piece(br, column), b_send, b_recv, column)
    at_distance(columns - 1, crossed)
    near_far_row = lax.rem(near_row + rows // 2, rows)
    for c in range(columns):
        remote(band(near_row, c), near_send.at[0, c], near_recv.at[0, c], near).wait_recv()
        remote(band(near_far_row, c), near_send.at[1, c], near_recv.at[1, c], near).wait_recv()
    for c in range(columns):
        remote(band(row, c), far_send.at[c], far_recv.at[c], far).wait_send()
        remote(band(row, c), near_send.at[0, c], near_recv.at[0, c], near).wait_send()
        remote(band(far_row, c), near_send.at[1, c], near_recv.at[1, c], near).wait_send()
        passed(band(row, c), line_send, line_recv, c)

    root = row == column
    relay = far_row == column
    from_far = relay
    from_near = jnp.logical_not(root | relay)

    def give(c):
        @pl.when(root)
        def _():
            for slot, to in ((0, far), (1, near)):
                pltpu.make_async_remote_copy(
                    src_ref=piece(br, c), dst_ref=piece(bc, c), send_sem=c_send.at[slot, c],
                    recv_sem=c_recv.at[c], device_id=to, device_id_type=pl.DeviceIdType.MESH,
                ).start()

    def take(c):
        remote(piece(br, c), b_send.at[0, c], b_recv.at[c], right).wait_recv()
        pass_on(piece(br, c), b_send, b_recv, c)
        give(c)

    def forward(c):
        @pl.when(relay)
        def _():
            remote(piece(bc, c), c_send.at[0, c], c_recv.at[c], far).wait_recv()
            remote(piece(bc, c), c_send.at[1, c], c_recv.at[c], near).start()

    give(column)
    between = {}
    between[1] = [functools.partial(at_distance, 1, take)]
    between[2] = [functools.partial(forward, column)]
    between[3] = [functools.partial(at_distance, 2, take)]
    between[4] = [functools.partial(at_distance, 1, forward)]
    between[5] = [functools.partial(at_distance, d, take) for d in range(3, columns)]
    between[6] = [functools.partial(at_distance, d, forward) for d in range(2, columns)]
    factor_in_place(a, w, between)
    for c in range(columns):
        @pl.when(from_near)
        def _(c=c):
            remote(piece(bc, c), c_send.at[0, c], c_recv.at[c], near).wait_recv()

        @pl.when(relay)
        def _(c=c):
            remote(piece(bc, c), c_send.at[1, c], c_recv.at[c], near).wait_send()

        @pl.when(root)
        def _(c=c):
            remote(piece(br, c), c_send.at[0, c], c_recv.at[c], far).wait_send()
            remote(piece(br, c), c_send.at[1, c], c_recv.at[c], near).wait_send()

        passed(piece(br, c), b_send, b_recv, c)

    @pl.when(root)
    def _():
        bc[...] = br[...]


def gather_factor_call(diag, lower, rows, columns):
    n = diag.shape[1]
    q = lower.shape[0] * columns
    dma = pltpu.SemaphoreType.DMA
    return pl.pallas_call(
        functools.partial(gather_factor_kernel, rows, columns),
        name="gather_factor",
        out_shape=(
            jax.ShapeDtypeStruct((n, n), F32),
            jax.ShapeDtypeStruct((n // BLOCK, BLOCK, BLOCK), F32),
            jax.ShapeDtypeStruct((q, n), F32),
            jax.ShapeDtypeStruct((q, n), F32),
        ),
        in_specs=[pl.BlockSpec(memory_space=pl.ANY)] * 2,
        out_specs=(VMEM,) * 4,
        scratch_shapes=[
            dma((2,)), dma((2, columns)), dma((columns,)), dma((columns,)), dma((columns,)),
            dma((2, columns)), dma((2, columns)), dma((2, columns)), dma((columns,)),
            dma((2, columns)), dma((columns,)),
        ],
        compiler_params=pltpu.CompilerParams(
            vmem_limit_bytes=40 << 20, collective_id=0, has_side_effects=True
        ),
    )(diag, lower)


def update_kernel(
    owners, slots, quarter, map_ref, l_ref, w_ref, br_ref, bc_ref, t_ref,
    panel_ref, out_ref, source_ref, xh, xl, lh, ll,
):
    n = l_ref.shape[0]
    q = br_ref.shape[0]
    share = panel_ref.shape[0]
    child = lax.axis_index("wide")
    row = lax.axis_index("grow")
    column = lax.axis_index("gcol")
    blocks = q // BLOCK
    per_owner = quarter // owners
    tile = 2 * BLOCK
    sides = (br_ref, bc_ref)
    lh[...], ll[...] = parts(l_ref[...])
    for k in range(n // BLOCK):
        low, high = k * BLOCK, k * BLOCK + BLOCK
        wk = parts(w_ref[k])

        def solve(i, carry, low=low, high=high, wk=wk):
            o = pl.multiple_of(i * tile, tile)
            for side, b in enumerate(sides):
                rest = b[pl.ds(o, tile), low:high]
                at = pl.ds(side * q + o, tile)
                if low:
                    rest = rest - split_dot(
                        (xh[at, :low], xl[at, :low]), (lh[low:high, :low], ll[low:high, :low]), NT
                    )
                x = split_dot(parts(rest), wk, NT)
                xh[at, low:high], xl[at, low:high] = parts(x)
                if side == 0:
                    br_ref[pl.ds(o, tile), low:high] = x
            return carry

        lax.fori_loop(0, q // tile, solve, 0)
    panel_ref[...] = br_ref[pl.ds(pl.multiple_of(column * share, share), share), :]

    def clear(i, carry):
        source_ref[i] = -1
        return carry

    lax.fori_loop(0, owners * per_owner, clear, 0)

    def place(g, carry):
        for b in range(blocks):
            to = map_ref[g, row * blocks + b] % quarter
            rank = jnp.int32(0)
            for e in range(b):
                other = map_ref[g, row * blocks + e] % quarter
                rank += (other // per_owner == to // per_owner).astype(jnp.int32)

            @pl.when(to // per_owner == child)
            def _(to=to, rank=rank):
                source_ref[g * per_owner + to % per_owner] = rank

        return carry

    lax.fori_loop(0, owners, place, 0)

    for b in range(blocks):
        o = b * BLOCK
        to = (map_ref[child, row * blocks + b] % quarter) // per_owner
        rank = jnp.int32(0)
        for e in range(b):
            other = (map_ref[child, row * blocks + e] % quarter) // per_owner
            rank += (other == to).astype(jnp.int32)
        out_ref[to * slots + rank] = t_ref[o : o + BLOCK, :] - split_dot(
            (xh[o : o + BLOCK, :], xl[o : o + BLOCK, :]), (xh[q:, :], xl[q:, :]), NT
        )


def update_call(row_map, factor, inverses, b_row, b_col, trailing, share, owners, slots, quarter):
    n = factor.shape[0]
    q = b_row.shape[0]
    return pl.pallas_call(
        functools.partial(update_kernel, owners, slots, quarter),
        name="update",
        out_shape=(
            jax.ShapeDtypeStruct((share, n), F32),
            jax.ShapeDtypeStruct((owners * slots, BLOCK, q), F32),
            jax.ShapeDtypeStruct((quarter,), jnp.int32),
        ),
        in_specs=[SMEM] + [VMEM] * 5,
        out_specs=(VMEM, VMEM, SMEM),
        scratch_shapes=[
            pltpu.VMEM((2 * q, n), BF16),
            pltpu.VMEM((2 * q, n), BF16),
            pltpu.VMEM((n, n), BF16),
            pltpu.VMEM((n, n), BF16),
        ],
        compiler_params=pltpu.CompilerParams(vmem_limit_bytes=56 << 20),
    )(row_map, factor, inverses, b_row, b_col, trailing)


def add_kernel(owners, map_ref, source_ref, parent_ref, in_ref, out_ref):
    p, g = pl.program_id(0), pl.program_id(1)
    per_owner = pl.num_programs(0)
    blocks = in_ref.shape[2] // BLOCK
    column_blocks = out_ref.shape[2] // BLOCK
    column = lax.axis_index("gcol")

    @pl.when(g == 0)
    def _():
        out_ref[...] = parent_ref[...]

    @pl.when(source_ref[g * per_owner + p] >= 0)
    def _():
        for b in range(blocks):
            to = map_ref[g, column * blocks + b] % column_blocks
            at = pl.ds(pl.multiple_of(to * BLOCK, BLOCK), BLOCK)
            out_ref[0, :, at] += in_ref[0, :, b * BLOCK : b * BLOCK + BLOCK]


def add_call(row_map, source, parent, incoming, owners, slots):
    _, rows, width = parent.shape
    per_owner = rows // BLOCK

    def pick(p, g, map_ref, source_ref):
        return (g * slots + jnp.maximum(source_ref[g * per_owner + p], 0), 0, 0)

    block = pl.BlockSpec((1, BLOCK, width), lambda p, g, *_: (0, p, 0))
    return pl.pallas_call(
        functools.partial(add_kernel, owners),
        name="extend_add",
        out_shape=jax.ShapeDtypeStruct(parent.shape, F32),
        grid_spec=pltpu.PrefetchScalarGridSpec(
            num_scalar_prefetch=2,
            grid=(per_owner, owners),
            in_specs=[block, pl.BlockSpec((1, BLOCK, incoming.shape[2]), pick)],
            out_specs=block,
        ),
        compiler_params=pltpu.CompilerParams(vmem_limit_bytes=32 << 20),
    )(row_map, source, parent, incoming)


def body(diag_block, lower_block, trailing_block, parent_front, row_map):
    owners = lax.axis_size("wide")
    rows, columns = lax.axis_size("grow"), lax.axis_size("gcol")
    share = diag_block.shape[1]
    row, column = lax.axis_index("grow"), lax.axis_index("gcol")
    factor, inverses, b_row, b_col = gather_factor_call(
        diag_block[0], lower_block[0], rows, columns
    )
    factor_rows = lax.dynamic_slice_in_dim(factor, (row * columns + column) * share, share, 0)
    quarter = parent_front.shape[1] * owners // BLOCK
    blocks = trailing_block.shape[1] // BLOCK
    slots = min(blocks, quarter // owners)
    panel, outgoing, source = update_call(
        row_map, factor, inverses, b_row, b_col, trailing_block[0],
        lower_block.shape[1], owners, slots, quarter,
    )
    incoming = lax.all_to_all(outgoing, "wide", split_axis=0, concat_axis=0, tiled=True)
    parent = add_call(row_map, source, parent_front, incoming, owners, slots)
    return (factor_rows[None], panel[None], parent)


def solution(mesh):
    placed = (
        P("wide", ("grow", "gcol"), None),
        P("wide", ("grow", "gcol"), None),
        P("wide", "grow", "gcol"),
        P("grow", "wide", "gcol"),
        P(),
    )
    return jax.shard_map(
        body,
        mesh=mesh,
        in_specs=placed,
        out_specs=(
            P("wide", ("grow", "gcol"), None),
            P("wide", ("grow", "gcol"), None),
            P("grow", "wide", "gcol"),
        ),
        check_vma=False,
    )
```

```python
import functools

import jax
import jax.numpy as jnp
from jax import lax
from jax.experimental import pallas as pl
from jax.experimental.pallas import tpu as pltpu
from jax.sharding import PartitionSpec as P

BLOCK = 128
HALF = 64
F32 = jnp.float32
BF16 = jnp.bfloat16
NT = (((1,), (1,)), ((), ()))
NN = (((1,), (0,)), ((), ()))
VMEM = pl.BlockSpec(memory_space=pltpu.VMEM)
SMEM = pl.BlockSpec(memory_space=pltpu.SMEM)


def full_dot(a, b, dims):
    return lax.dot_general(
        a, b, dims, precision=lax.Precision.HIGHEST, preferred_element_type=F32
    )


def parts(x):
    high = x.astype(BF16)
    return high, (x - high.astype(F32)).astype(BF16)


def split_dot(a, b, dims):
    one = functools.partial(lax.dot_general, dimension_numbers=dims, preferred_element_type=F32)
    return one(a[0], b[0]) + (one(a[0], b[1]) + one(a[1], b[0]))


def factor_half(block):
    half = block.shape[0]
    rows = lax.broadcasted_iota(jnp.int32, (half, half), 0)
    cols = lax.broadcasted_iota(jnp.int32, (half, half), 1)
    eye = jnp.where(rows == cols, 1.0, 0.0).astype(F32)
    full = jnp.concatenate([block, eye], axis=1)
    count = half // 8
    wide = (8, 2 * half)
    groups = [full[8 * s : 8 * s + 8] for s in range(count)]
    sub = lax.broadcasted_iota(jnp.int32, wide, 0)
    done = []
    for s in range(count):
        c = 8 * s
        spread = lambda x: jnp.broadcast_to(x, wide)
        lead = [spread(groups[s][i : i + 1, :]) for i in range(8)]
        pivot = {
            (i, j): spread(lead[i][:, c + j : c + j + 1]) for i in range(8) for j in range(i, 8)
        }
        below = range(s + 1, count)
        column = {t: [spread(groups[t][:, c + j : c + j + 1]) for j in range(8)] for t in below}
        keep = jnp.zeros(wide, F32)
        for j in range(8):
            r = lax.rsqrt(pivot[j, j])
            unit = lead[j] * r
            mult = {i: pivot[j, i] * r for i in range(j + 1, 8)}
            for i in range(j + 1, 8):
                for q in range(i, 8):
                    pivot[i, q] = pivot[i, q] - mult[i] * mult[q]
                lead[i] = lead[i] - mult[i] * unit
            for t in below:
                m = column[t][j] * r
                for i in range(j + 1, 8):
                    column[t][i] = column[t][i] - m * mult[i]
                groups[t] = groups[t] - m * unit
            keep = jnp.where(sub == j, unit, keep)
        done.append(keep)
    both = jnp.concatenate(done, axis=0)
    upper = jnp.where(rows <= cols, both[:, :half], 0.0)
    inverse = jnp.where(rows >= cols, both[:, half:], 0.0)
    return upper.T, inverse


def square(a, b, c):
    return jnp.concatenate(
        [
            jnp.concatenate([a, jnp.zeros_like(a)], axis=1),
            jnp.concatenate([b, c], axis=1),
        ],
        axis=0,
    )


def factor_in_place(a, w, between):
    n = a.shape[0]
    count = n // BLOCK

    def step(k, carry):
        o = pl.multiple_of(k * BLOCK, BLOCK)
        d = a[pl.ds(o, BLOCK), pl.ds(o, BLOCK)]
        l1, w1 = factor_half(d[:HALF, :HALF])
        l21 = full_dot(d[HALF:, :HALF], w1, NT)
        l2, w2 = factor_half(d[HALF:, HALF:] - full_dot(l21, l21, NT))
        w21 = -full_dot(w2, full_dot(l21, w1, NN), NN)
        a[pl.ds(o, BLOCK), pl.ds(o, BLOCK)] = square(l1, l21, l2)
        w[k] = square(w1, w21, w2)
        for at in range(count - 1):

            @pl.when(k == at)
            def _(at=at):
                low, high = at * BLOCK, at * BLOCK + BLOCK
                a[low:high, high:] = jnp.zeros((BLOCK, n - high), F32)
                p = full_dot(a[high:, low:high], w[at], NT)
                a[high:, low:high] = p
                for c in range(high, n, 2 * BLOCK):
                    e = min(c + 2 * BLOCK, n)
                    a[c:, c:e] = a[c:, c:e] - full_dot(p[c - high :], p[c - high : e - high], NT)
                for act in between.get(at, ()):
                    act()

        return carry

    lax.fori_loop(0, count, step, 0)


def gather_factor_kernel(
    rows, columns, d_ref, x_ref, a, w, br, bc,
    local, line_send, line_recv, far_send, far_recv, near_send, near_recv,
    b_send, b_recv, c_send, c_recv,
):
    row, column = lax.axis_index("grow"), lax.axis_index("gcol")
    far_row = lax.rem(row + rows // 2, rows)
    near_row = row + 1 - 2 * lax.rem(row, 2)
    right, left = {"gcol": column + 1}, {"gcol": column - 1}
    far, near = {"grow": far_row}, {"grow": near_row}
    share, part = d_ref.shape[0], x_ref.shape[0]
    has_left, has_right = column > 0, column < columns - 1

    def band(r, c):
        return a.at[pl.ds(pl.multiple_of((r * columns + c) * share, share), share)]

    def piece(ref, c):
        return ref.at[pl.ds(pl.multiple_of(c * part, part), part)]

    def remote(ref, send, recv, to):
        return pltpu.make_async_remote_copy(
            src_ref=ref, dst_ref=ref, send_sem=send, recv_sem=recv,
            device_id=to, device_id_type=pl.DeviceIdType.MESH,
        )

    own_d = pltpu.make_async_copy(d_ref, band(row, column), local.at[0])
    own_x = pltpu.make_async_copy(x_ref, piece(br, column), local.at[1])
    own_d.start()
    own_x.start()
    barrier = pltpu.get_barrier_semaphore()
    next_column = {"gcol": lax.rem(column + 1, columns)}
    last_column = {"gcol": lax.rem(column + columns - 1, columns)}
    for to in (far, near, next_column, last_column):
        pl.semaphore_signal(barrier, inc=1, device_id=to, device_id_type=pl.DeviceIdType.MESH)
    pl.semaphore_wait(barrier, 4)
    own_d.wait()
    own_x.wait()

    def pass_on(ref, send, recv, c, both=False):
        @pl.when((c <= column) & has_right)
        def _():
            remote(ref, send.at[0, c], recv.at[c], right).start()

        @pl.when((c >= column) & has_left)
        def _():
            remote(ref, send.at[1, c], recv.at[c], left).start()

    def passed(ref, send, recv, c):
        @pl.when((c <= column) & has_right)
        def _():
            remote(ref, send.at[0, c], recv.at[c], right).wait_send()

        @pl.when((c >= column) & has_left)
        def _():
            remote(ref, send.at[1, c], recv.at[c], left).wait_send()

    def at_distance(d, act):
        for c, there in ((column - d, column - d >= 0), (column + d, column + d < columns)):
            pl.when(there)(functools.partial(act, c))

    def spread(c):
        remote(band(row, c), far_send.at[c], far_recv.at[c], far).start()
        remote(band(row, c), near_send.at[0, c], near_recv.at[0, c], near).start()

    pass_on(band(row, column), line_send, line_recv, column)
    spread(column)

    def arrived(c):
        remote(band(row, c), line_send.at[0, c], line_recv.at[c], right).wait_recv()
        pass_on(band(row, c), line_send, line_recv, c)
        spread(c)

    def crossed(c):
        remote(band(far_row, c), far_send.at[c], far_recv.at[c], far).wait_recv()
        remote(band(far_row, c), near_send.at[1, c], near_recv.at[1, c], near).start()

    at_distance(1, arrived)
    crossed(column)
    for d in range(2, columns):
        at_distance(d, arrived)
        at_distance(d - 1, crossed)
    pass_on(piece(br, column), b_send, b_recv, column)
    at_distance(columns - 1, crossed)
    near_far_row = lax.rem(near_row + rows // 2, rows)
    for c in range(columns):
        remote(band(near_row, c), near_send.at[0, c], near_recv.at[0, c], near).wait_recv()
        remote(band(near_far_row, c), near_send.at[1, c], near_recv.at[1, c], near).wait_recv()
    for c in range(columns):
        remote(band(row, c), far_send.at[c], far_recv.at[c], far).wait_send()
        remote(band(row, c), near_send.at[0, c], near_recv.at[0, c], near).wait_send()
        remote(band(far_row, c), near_send.at[1, c], near_recv.at[1, c], near).wait_send()
        passed(band(row, c), line_send, line_recv, c)

    root = row == column
    relay = far_row == column
    from_far = relay
    from_near = jnp.logical_not(root | relay)

    def give(c):
        @pl.when(root)
        def _():
            for slot, to in ((0, far), (1, near)):
                pltpu.make_async_remote_copy(
                    src_ref=piece(br, c), dst_ref=piece(bc, c), send_sem=c_send.at[slot, c],
                    recv_sem=c_recv.at[c], device_id=to, device_id_type=pl.DeviceIdType.MESH,
                ).start()

    def take(c):
        remote(piece(br, c), b_send.at[0, c], b_recv.at[c], right).wait_recv()
        pass_on(piece(br, c), b_send, b_recv, c)
        give(c)

    def forward(c):
        @pl.when(relay)
        def _():
            remote(piece(bc, c), c_send.at[0, c], c_recv.at[c], far).wait_recv()
            remote(piece(bc, c), c_send.at[1, c], c_recv.at[c], near).start()

    give(column)
    between = {}
    between[1] = [functools.partial(at_distance, 1, take)]
    between[2] = [functools.partial(forward, column)]
    between[3] = [functools.partial(at_distance, 2, take)]
    between[4] = [functools.partial(at_distance, 1, forward)]
    between[5] = [functools.partial(at_distance, d, take) for d in range(3, columns)]
    between[6] = [functools.partial(at_distance, d, forward) for d in range(2, columns)]
    factor_in_place(a, w, between)
    for c in range(columns):
        @pl.when(from_near)
        def _(c=c):
            remote(piece(bc, c), c_send.at[0, c], c_recv.at[c], near).wait_recv()

        @pl.when(relay)
        def _(c=c):
            remote(piece(bc, c), c_send.at[1, c], c_recv.at[c], near).wait_send()

        @pl.when(root)
        def _(c=c):
            remote(piece(br, c), c_send.at[0, c], c_recv.at[c], far).wait_send()
            remote(piece(br, c), c_send.at[1, c], c_recv.at[c], near).wait_send()

        passed(piece(br, c), b_send, b_recv, c)

    @pl.when(root)
    def _():
        bc[...] = br[...]


def gather_factor_call(diag, lower, rows, columns):
    n = diag.shape[1]
    q = lower.shape[0] * columns
    dma = pltpu.SemaphoreType.DMA
    return pl.pallas_call(
        functools.partial(gather_factor_kernel, rows, columns),
        name="gather_factor",
        out_shape=(
            jax.ShapeDtypeStruct((n, n), F32),
            jax.ShapeDtypeStruct((n // BLOCK, BLOCK, BLOCK), F32),
            jax.ShapeDtypeStruct((q, n), F32),
            jax.ShapeDtypeStruct((q, n), F32),
        ),
        in_specs=[pl.BlockSpec(memory_space=pl.ANY)] * 2,
        out_specs=(VMEM,) * 4,
        scratch_shapes=[
            dma((2,)), dma((2, columns)), dma((columns,)), dma((columns,)), dma((columns,)),
            dma((2, columns)), dma((2, columns)), dma((2, columns)), dma((columns,)),
            dma((2, columns)), dma((columns,)),
        ],
        compiler_params=pltpu.CompilerParams(
            vmem_limit_bytes=40 << 20, collective_id=0, has_side_effects=True
        ),
    )(diag, lower)


def update_kernel(
    owners, slots, quarter, map_ref, l_ref, w_ref, br_ref, bc_ref, t_ref,
    panel_ref, out_ref, source_ref, xh, xl, lh, ll,
):
    n = l_ref.shape[0]
    q = br_ref.shape[0]
    share = panel_ref.shape[0]
    child = lax.axis_index("wide")
    row = lax.axis_index("grow")
    column = lax.axis_index("gcol")
    blocks = q // BLOCK
    per_owner = quarter // owners
    tile = 2 * BLOCK
    sides = (br_ref, bc_ref)
    lh[...], ll[...] = parts(l_ref[...])
    pair = 2 * BLOCK
    for k in range(n // pair):
        low, high = k * pair, k * pair + pair
        wa, wb = w_ref[2 * k], w_ref[2 * k + 1]
        across = l_ref[low + BLOCK : high, low : low + BLOCK]
        wk = parts(square(wa, -full_dot(wb, full_dot(across, wa, NN), NN), wb))

        def solve(i, carry, low=low, high=high, wk=wk):
            o = pl.multiple_of(i * tile, tile)
            for side, b in enumerate(sides):
                rest = b[pl.ds(o, tile), low:high]
                at = pl.ds(side * q + o, tile)
                if low:
                    rest = rest - split_dot(
                        (xh[at, :low], xl[at, :low]), (lh[low:high, :low], ll[low:high, :low]), NT
                    )
                x = split_dot(parts(rest), wk, NT)
                xh[at, low:high], xl[at, low:high] = parts(x)
                if side == 0:
                    br_ref[pl.ds(o, tile), low:high] = x
            return carry

        lax.fori_loop(0, q // tile, solve, 0)
    panel_ref[...] = br_ref[pl.ds(pl.multiple_of(column * share, share), share), :]

    def clear(i, carry):
        source_ref[i] = -1
        return carry

    lax.fori_loop(0, owners * per_owner, clear, 0)

    def place(g, carry):
        for b in range(blocks):
            to = map_ref[g, row * blocks + b] % quarter
            rank = jnp.int32(0)
            for e in range(b):
                other = map_ref[g, row * blocks + e] % quarter
                rank += (other // per_owner == to // per_owner).astype(jnp.int32)

            @pl.when(to // per_owner == child)
            def _(to=to, rank=rank):
                source_ref[g * per_owner + to % per_owner] = rank

        return carry

    lax.fori_loop(0, owners, place, 0)

    step = 3 if blocks % 3 == 0 else 1
    for first in range(0, blocks, step):
        low, high = first * BLOCK, (first + step) * BLOCK
        update = split_dot((xh[low:high, :], xl[low:high, :]), (xh[q:, :], xl[q:, :]), NT)
        for b in range(first, first + step):
            o = b * BLOCK
            to = (map_ref[child, row * blocks + b] % quarter) // per_owner
            rank = jnp.int32(0)
            for e in range(b):
                other = (map_ref[child, row * blocks + e] % quarter) // per_owner
                rank += (other == to).astype(jnp.int32)
            out_ref[to * slots + rank] = (
                t_ref[o : o + BLOCK, :] - update[o - low : o - low + BLOCK, :]
            )


def update_call(row_map, factor, inverses, b_row, b_col, trailing, share, owners, slots, quarter):
    n = factor.shape[0]
    q = b_row.shape[0]
    return pl.pallas_call(
        functools.partial(update_kernel, owners, slots, quarter),
        name="update",
        out_shape=(
            jax.ShapeDtypeStruct((share, n), F32),
            jax.ShapeDtypeStruct((owners * slots, BLOCK, q), F32),
            jax.ShapeDtypeStruct((quarter,), jnp.int32),
        ),
        in_specs=[SMEM] + [VMEM] * 5,
        out_specs=(VMEM, VMEM, SMEM),
        scratch_shapes=[
            pltpu.VMEM((2 * q, n), BF16),
            pltpu.VMEM((2 * q, n), BF16),
            pltpu.VMEM((n, n), BF16),
            pltpu.VMEM((n, n), BF16),
        ],
        compiler_params=pltpu.CompilerParams(vmem_limit_bytes=56 << 20),
    )(row_map, factor, inverses, b_row, b_col, trailing)


def add_kernel(owners, map_ref, source_ref, parent_ref, in_ref, out_ref):
    p, g = pl.program_id(0), pl.program_id(1)
    per_owner = pl.num_programs(0)
    blocks = in_ref.shape[2] // BLOCK
    column_blocks = out_ref.shape[2] // BLOCK
    column = lax.axis_index("gcol")

    @pl.when(g == 0)
    def _():
        out_ref[...] = parent_ref[...]

    @pl.when(source_ref[g * per_owner + p] >= 0)
    def _():
        for b in range(blocks):
            to = map_ref[g, column * blocks + b] % column_blocks
            at = pl.ds(pl.multiple_of(to * BLOCK, BLOCK), BLOCK)
            out_ref[0, :, at] += in_ref[0, :, b * BLOCK : b * BLOCK + BLOCK]


def add_call(row_map, source, parent, incoming, owners, slots):
    _, rows, width = parent.shape
    per_owner = rows // BLOCK

    def pick(p, g, map_ref, source_ref):
        return (g * slots + jnp.maximum(source_ref[g * per_owner + p], 0), 0, 0)

    block = pl.BlockSpec((1, BLOCK, width), lambda p, g, *_: (0, p, 0))
    return pl.pallas_call(
        functools.partial(add_kernel, owners),
        name="extend_add",
        out_shape=jax.ShapeDtypeStruct(parent.shape, F32),
        grid_spec=pltpu.PrefetchScalarGridSpec(
            num_scalar_prefetch=2,
            grid=(per_owner, owners),
            in_specs=[block, pl.BlockSpec((1, BLOCK, incoming.shape[2]), pick)],
            out_specs=block,
        ),
        compiler_params=pltpu.CompilerParams(vmem_limit_bytes=32 << 20),
    )(row_map, source, parent, incoming)


def body(diag_block, lower_block, trailing_block, parent_front, row_map):
    owners = lax.axis_size("wide")
    rows, columns = lax.axis_size("grow"), lax.axis_size("gcol")
    share = diag_block.shape[1]
    row, column = lax.axis_index("grow"), lax.axis_index("gcol")
    factor, inverses, b_row, b_col = gather_factor_call(
        diag_block[0], lower_block[0], rows, columns
    )
    factor_rows = lax.dynamic_slice_in_dim(factor, (row * columns + column) * share, share, 0)
    quarter = parent_front.shape[1] * owners // BLOCK
    blocks = trailing_block.shape[1] // BLOCK
    slots = min(blocks, quarter // owners)
    panel, outgoing, source = update_call(
        row_map, factor, inverses, b_row, b_col, trailing_block[0],
        lower_block.shape[1], owners, slots, quarter,
    )
    incoming = lax.all_to_all(outgoing, "wide", split_axis=0, concat_axis=0, tiled=True)
    parent = add_call(row_map, source, parent_front, incoming, owners, slots)
    return (factor_rows[None], panel[None], parent)


def solution(mesh):
    placed = (
        P("wide", ("grow", "gcol"), None),
        P("wide", ("grow", "gcol"), None),
        P("wide", "grow", "gcol"),
        P("grow", "wide", "gcol"),
        P(),
    )
    return jax.shard_map(
        body,
        mesh=mesh,
        in_specs=placed,
        out_specs=(
            P("wide", ("grow", "gcol"), None),
            P("wide", ("grow", "gcol"), None),
            P("grow", "wide", "gcol"),
        ),
        check_vma=False,
    )
```
